32 devices in a mesh: outer: 8 (over z, y), inner: 4 (over x, core).
Axes of the slice: x: 2, y: 2, z: 4, core: 2. Of those that a mesh axis runs over, the one named last changes fastest.
Arguments:
- x_in: bfloat16 [4096, 8192], P(('outer', 'inner')), may hold values from -6 to 6
- gate_in: bfloat16 [4096, 8192], P(('outer', 'inner')), may hold values from -6 to 6
- conv_weight: float32 [4, 8192], replicated, may hold values from -3 to 3
- conv_bias: float32 [8192], replicated, may hold values from -3 to 3
- x_proj: bfloat16 [8192, 288], replicated, may hold values from -0.0625 to 0.0625
- dt_proj: bfloat16 [256, 8192], replicated, may hold values from -0.375 to 0.375
- dt_bias: float32 [8192], replicated, may hold values from -9 to -2
- decay_rates: float32 [16, 8192], replicated, may hold values from 1 to 16
- skip_gain: float32 [8192], replicated, may hold values from 0.5 to 1.5
Outputs:
- gated_out: bfloat16 [4096, 8192], P(('outer', 'inner'))
The draws below stay inside these ranges and needn't reach their ends.
All inputs are finite; a program needn't handle non-finite values.
Results may differ from the reference program's by a relative error of at most 0.0085.
Values may be sent and summed in bfloat16 or wider, within the bound.
No kernel may reach another device: no remote copies, remote signals or barrier semaphores. Data moves between devices by JAX's collectives and lax.ppermute only.
A program may use at most 192 MiB of HBM per device.

```python
import math
import jax
import jax.numpy as jnp
from jax import lax

E = 8192
N = 16
R = 256
KW = 4
TOKENS = 4096


def level_of(stream_key, shape, cuts, low, high):
    def one(position, parts):
        draws = jax.random.uniform(jax.random.fold_in(jax.random.fold_in(stream_key, 6), position), (parts,), jnp.float32, low / len(cuts), high / len(cuts))
        return jnp.repeat(jnp.exp(draws), shape[position] // parts).reshape((-1,) + (1,) * (len(shape) - position - 1))

    level = one(*cuts[0])
    for cut in cuts[1:]:
        level = level * one(*cut)
    return level


def scatter_about(key, shape, scale, bound, shards=(), kind=jnp.bfloat16):
    level = level_of(key, shape, shards, -0.22, 0.18) if shards else 1.0
    entries = jax.random.normal(key, shape, jnp.float32) * scale * level
    return jnp.minimum(jnp.maximum(entries, -bound), bound).astype(kind)


def setup_inputs(seed: int = 0) -> dict:
    key_list = jax.random.split(jax.random.key(seed), 10)
    x_in = scatter_about(key_list[0], (TOKENS, E), 1.0, 6.0, ((0, 32),))
    gate_in = scatter_about(key_list[1], (TOKENS, E), 1.0, 6.0, ((0, 32),))
    conv_weight = scatter_about(key_list[2], (KW, E), KW ** -0.5, 3.0, (), jnp.float32)
    conv_bias = scatter_about(key_list[3], (E,), 0.5, 3.0, (), jnp.float32)
    x_proj = scatter_about(key_list[4], (E, R + 2 * N), E ** -0.5, 0.0625)
    dt_proj = scatter_about(key_list[5], (R, E), R ** -0.5, 0.375)
    dt_bias = jnp.clip(jax.random.uniform(key_list[6], (E,), jnp.float32, -9.0, -2.0), -9.0, -2.0)
    decay_rates = jnp.clip(jnp.exp(jax.random.uniform(key_list[7], (N, E), jnp.float32, math.log(1.0), math.log(16.0))), 1.0, 16.0)
    skip_gain = jnp.clip(1.0 + 0.1 * jax.random.normal(key_list[8], (E,), jnp.float32), 0.5, 1.5)
    return dict(x_in=x_in, gate_in=gate_in, conv_weight=conv_weight, conv_bias=conv_bias, x_proj=x_proj, dt_proj=dt_proj, dt_bias=dt_bias, decay_rates=decay_rates, skip_gain=skip_gain)


dt_ceiling = 0.25


def reference(x_in, gate_in, conv_weight, conv_bias, x_proj, dt_proj, dt_bias, decay_rates, skip_gain):
    length = x_in.shape[0]
    width = x_in.shape[1]
    taps = conv_weight.shape[0]
    xfloat = x_in.astype(jnp.float32)
    padded = jnp.concatenate([jnp.zeros((taps - 1, width), jnp.float32), xfloat], axis=0)
    conv = conv_bias[None, :]
    for k in range(taps):
        conv = conv + conv_weight[k][None, :] * padded[k:k + length]
    u_act = jax.nn.silu(conv).astype(jnp.bfloat16)
    proj = jnp.dot(u_act, x_proj, preferred_element_type=jnp.float32)
    rank = dt_proj.shape[0]
    states = decay_rates.shape[0]
    dt_low = proj[:, :rank].astype(jnp.bfloat16)
    bmat = proj[:, rank:rank + states]
    cmat = proj[:, rank + states:]
    step_size = jnp.minimum(jax.nn.softplus(jnp.dot(dt_low, dt_proj, preferred_element_type=jnp.float32) + dt_bias[None, :]), dt_ceiling)
    ufloat = u_act.astype(jnp.float32)

    def advance(state, inputs):
        dt_row, u_row, b_row, c_row = inputs
        state = jnp.exp(-dt_row[None, :] * decay_rates) * state + b_row[:, None] * (dt_row * u_row)[None, :]
        return state, jnp.sum(c_row[:, None] * state, axis=0)

    start = jnp.zeros((states, width), jnp.float32)
    final, outputs = lax.scan(advance, start, (step_size, ufloat, bmat, cmat))
    y_full = outputs + skip_gain[None, :] * ufloat
    return (y_full * jax.nn.silu(gate_in.astype(jnp.float32))).astype(jnp.bfloat16)
```

```python
import jax
import jax.numpy as jnp
from jax import lax
from jax.experimental import pallas as pl
from jax.experimental.pallas import tpu as pltpu
from jax.sharding import PartitionSpec as P

AXES = ("outer", "inner")
LOG2E = 1.4426950408889634
DT_CEILING = 0.25
GROUP = 16
LANES = 128
F32 = jnp.float32
BF16 = jnp.bfloat16


def silu(value):
    half = 0.5 * value
    return half + half * jnp.tanh(half)


def capped_softplus(value):
    z = jnp.exp(jnp.minimum(value, -1.0))
    w = 1.0 + z
    return jnp.minimum(jnp.log(w) + (z - (w - 1.0)), DT_CEILING)


def pick_block(width, limit):
    block = limit
    while width % block:
        block //= 2
    return block


def spread_c(cmat, states, by_token):
    rows = cmat.shape[0]
    wide = GROUP * states
    n = lax.broadcasted_iota(jnp.int32, (states, wide), 0)
    col = lax.broadcasted_iota(jnp.int32, (states, wide), 1)
    pick = col % states if by_token else col // GROUP
    select = jnp.where(n == pick, 1.0, 0.0).astype(BF16)
    spread = jnp.dot(cmat.astype(BF16), select, preferred_element_type=F32)
    t = lax.broadcasted_iota(jnp.int32, (rows, wide), 0) % GROUP
    col = lax.broadcasted_iota(jnp.int32, (rows, wide), 1)
    token = col // states if by_token else col % GROUP
    return jnp.where(t == token, spread, 0.0).astype(BF16)


class Share:
    def __init__(self, width, parts, states):
        self.width = width // parts
        self.lanes = min(self.width, LANES)
        self.strips = self.width // self.lanes
        self.states = states
        self.rows = states * self.strips
        self.message_rows = -(-(self.rows + 2 * self.strips) // 8) * 8


def front(x_in, halo, conv_weight, conv_bias, x_proj_t, dt_proj, dt_bias, decay, skip, share):
    rows, width = x_in.shape
    taps = conv_weight.shape[0]
    rank = dt_proj.shape[0]
    states = decay.shape[0]
    columns = x_proj_t.shape[0]
    block = pick_block(width, 512)
    count = width // block
    per_block = block // share.width
    groups = rows // GROUP

    def body(x_hbm, halo_ref, cw_ref, cb_ref, xp_hbm, dp_hbm, bias_ref, a_ref, skip_ref,
             y_hbm, cum_hbm, msg_ref, bc_ref,
             x_s, xp_s, dp_s, u_s, y_s, cum_s, proj, low, hl, b_s, c_s, dt_s, v_s, h0_s, h1_s, add0_s, add1_s,
             x_sem, xp_sem, dp_sem, y_sem, cum_sem):
        h_s = (h0_s, h1_s)
        add_s = (add0_s, add1_s)

        def at(j):
            return pl.ds(pl.multiple_of(j * block, block), block)

        def copies_in(j):
            return (
                pltpu.make_async_copy(x_hbm.at[:, at(j)], x_s.at[:, at(j)], x_sem.at[j]),
                pltpu.make_async_copy(xp_hbm.at[:, at(j)], xp_s.at[:, at(j)], xp_sem.at[j]),
            )

        def copy_dp(j):
            return pltpu.make_async_copy(dp_hbm.at[:, at(j)], dp_s.at[:, at(j)], dp_sem.at[j])

        def copies_out(j):
            return (
                pltpu.make_async_copy(y_s.at[:, at(j)], y_hbm.at[:, at(j)], y_sem.at[j]),
                pltpu.make_async_copy(cum_s.at[:, at(j)], cum_hbm.at[:, at(j)], cum_sem.at[j]),
            )

        for j in range(count):
            for copy in copies_in(j):
                copy.start()
        for j in range(count):
            copy_dp(j).start()
        proj[...] = jnp.zeros_like(proj)

        top = lax.broadcasted_iota(jnp.int32, (8, block), 0)

        def head(j, _):
            for copy in copies_in(j):
                copy.wait()
            lanes = at(j)
            x = x_s[:, lanes].astype(F32)
            before = halo_ref[:, lanes]
            conv = cb_ref[:, lanes] + cw_ref[taps - 1 : taps, lanes] * x
            for k in range(1, taps):
                moved = pltpu.roll(x, k, 0)
                start = jnp.where(top < k, pltpu.roll(before, k, 0), moved[:8])
                moved = jnp.concatenate([start, moved[8:]], axis=0)
                conv = conv + cw_ref[taps - 1 - k : taps - k, lanes] * moved
            u = silu(conv).astype(BF16)
            u_s[:, lanes] = u
            proj[...] += lax.dot_general(u, xp_s[:, lanes], (((1,), (1,)), ((), ())), preferred_element_type=F32)
            return 0

        lax.fori_loop(0, count, head, 0)

        low[...] = proj[:, :rank].astype(BF16)
        bmat = proj[:, rank : rank + states]
        cmat = proj[:, rank + states : rank + 2 * states]
        bc_ref[...] = proj[:, rank:]
        c_s[...] = spread_c(cmat, states, True)
        high = bmat.astype(BF16).astype(F32)
        hl[...] = jnp.zeros_like(hl)
        hl[:, :states] = high
        hl[:, states : 2 * states] = bmat - high
        n = lax.broadcasted_iota(jnp.int32, (states, LANES), 0)
        lane = lax.broadcasted_iota(jnp.int32, (states, LANES), 1)
        keep = jnp.logical_or(lane == n, lane == n + states)
        ones = jnp.ones((LANES, LANES), BF16)
        token = lax.broadcasted_iota(jnp.int32, (GROUP * states, LANES), 1)
        own = lax.broadcasted_iota(jnp.int32, (GROUP * states, LANES), 0) // states

        def fill(g, _):
            base = pl.multiple_of(g * GROUP, GROUP)
            picked = [
                jnp.where(keep, jnp.broadcast_to(hl[pl.ds(base + i, 1), :], (states, LANES)), 0.0).astype(BF16)
                for i in range(GROUP)
            ]
            spread = jnp.dot(jnp.concatenate(picked, axis=0), ones, preferred_element_type=F32)
            b_s[g] = jnp.where(token == own, spread, 0.0)[:, :GROUP].astype(BF16)
            return 0

        lax.fori_loop(0, groups, fill, 0)

        row = lax.broadcasted_iota(jnp.int32, (rows, rows), 0)
        col = lax.broadcasted_iota(jnp.int32, (rows, rows), 1)
        tri = jnp.where(row >= col, 1.0, 0.0).astype(BF16)
        fill_rows = share.message_rows - share.rows - 2 * share.strips

        def tail(j, _):
            lanes = at(j)
            copy_dp(j).wait()
            raw = jnp.dot(low[...], dp_s[:, lanes], preferred_element_type=F32)
            dt = capped_softplus(raw + bias_ref[:, lanes])
            dt_s[...] = dt
            v_s[...] = (dt * u_s[:, lanes].astype(F32)).astype(BF16)
            cum = jnp.dot(tri, dt.astype(BF16), preferred_element_type=F32)
            cum_s[:, lanes] = cum.astype(BF16)
            total = cum[rows - 1 : rows]
            rates = a_ref[:, lanes] * (-LOG2E)
            skip_row = skip_ref[:, lanes]

            def load(g):
                add_s[g % 2][...] = jnp.dot(
                    b_s[g], v_s[g * GROUP : (g + 1) * GROUP, :], preferred_element_type=F32
                )

            def scan_group(g, h):
                for i in range(GROUP):
                    t = g * GROUP + i
                    at_i = slice(i * states, (i + 1) * states)
                    dtb = jnp.broadcast_to(dt_s[t : t + 1, :], (states, block))
                    h = jnp.exp2(dtb * rates) * h + add_s[g % 2][at_i, :]
                    h_s[g % 2][at_i, :] = h.astype(BF16)
                return h

            def emit(g):
                tokens = slice(g * GROUP, (g + 1) * GROUP)
                y = jnp.dot(c_s[tokens, :], h_s[g % 2][...], preferred_element_type=F32)
                y_s[tokens, lanes] = y + skip_row * u_s[tokens, lanes].astype(F32)

            h = jnp.zeros((states, block), F32)
            load(0)
            for g in range(groups):
                if g + 1 < groups:
                    load(g + 1)
                if g > 0:
                    emit(g - 1)
                h = scan_group(g, h)
            emit(groups - 1)
            for copy in copies_out(j):
                copy.start()
            high = total.astype(BF16).astype(F32)
            rest = total - high
            for p in range(per_block):
                cuts = [
                    slice(p * share.width + s * share.lanes, p * share.width + (s + 1) * share.lanes)
                    for s in range(share.strips)
                ]
                pieces = [h[:, c] for c in cuts] + [high[:, c] for c in cuts] + [rest[:, c] for c in cuts]
                if fill_rows:
                    pieces.append(jnp.zeros((fill_rows, share.lanes), F32))
                msg_ref[j * per_block + p] = jnp.concatenate(pieces, axis=0).astype(BF16)
            return 0

        lax.fori_loop(0, count, tail, 0)
        for j in range(count):
            for copy in copies_out(j):
                copy.wait()

    whole = pl.BlockSpec(memory_space=pltpu.VMEM)
    held = pl.BlockSpec(memory_space=pl.ANY)
    return pl.pallas_call(
        body,
        in_specs=[held, whole, whole, whole, held, held, whole, whole, whole],
        out_specs=[held, held, whole, whole],
        out_shape=[
            jax.ShapeDtypeStruct((rows, width), F32),
            jax.ShapeDtypeStruct((rows, width), BF16),
            jax.ShapeDtypeStruct((width // share.width, share.message_rows, share.lanes), BF16),
            jax.ShapeDtypeStruct((rows, 2 * states), F32),
        ],
        scratch_shapes=[
            pltpu.VMEM((rows, width), BF16),
            pltpu.VMEM((columns, width), BF16),
            pltpu.VMEM((rank, width), BF16),
            pltpu.VMEM((rows, width), BF16),
            pltpu.VMEM((rows, width), F32),
            pltpu.VMEM((rows, width), BF16),
            pltpu.VMEM((rows, columns), F32),
            pltpu.VMEM((rows, rank), BF16),
            pltpu.VMEM((rows, LANES), F32),
            pltpu.VMEM((groups, GROUP * states, GROUP), BF16),
            pltpu.VMEM((rows, GROUP * states), BF16),
            pltpu.VMEM((rows, block), F32),
            pltpu.VMEM((rows, block), BF16),
            pltpu.VMEM((GROUP * states, block), BF16),
            pltpu.VMEM((GROUP * states, block), BF16),
            pltpu.VMEM((GROUP * states, block), F32),
            pltpu.VMEM((GROUP * states, block), F32),
        ]
        + [pltpu.SemaphoreType.DMA((count,))] * 5,
        compiler_params=pltpu.CompilerParams(vmem_limit_bytes=40 * 2**20),
        name="front",
    )(x_in, halo, conv_weight, conv_bias, x_proj_t, dt_proj, dt_bias, decay, skip)


def combine(message, rates, share):
    parts = message.shape[0]
    states = share.states

    def body(msg_ref, a_ref, h_ref):
        rates = [a_ref[:, s * share.lanes : (s + 1) * share.lanes] * (-LOG2E) for s in range(share.strips)]

        def one(p, carry):
            later = []
            for s, h in enumerate(carry):
                h_ref[p, s * states : (s + 1) * states, :] = h.astype(BF16)
                high = msg_ref[p, share.rows + s : share.rows + s + 1, :].astype(F32)
                at = share.rows + share.strips + s
                total = high + msg_ref[p, at : at + 1, :].astype(F32)
                add = msg_ref[p, s * states : (s + 1) * states, :].astype(F32)
                later.append(jnp.exp2(rates[s] * total) * h + add)
            return tuple(later)

        zero = jnp.zeros((states, share.lanes), F32)
        lax.fori_loop(0, parts, one, (zero,) * share.strips, unroll=8)

    return pl.pallas_call(
        body, out_shape=jax.ShapeDtypeStruct((parts, share.rows, share.lanes), BF16), name="combine"
    )(message, rates)


def final(cum, h_in, y, gate, bc, decay, share):
    rows, width = cum.shape
    states = decay.shape[0]
    block = pick_block(width, 1024)
    sub = pick_block(block, 256)
    count = width // block
    per_block = block // share.width

    def body(cum_ref, h_ref, y_ref, gate_ref, bc_ref, a_ref, out_ref, c_s, a_s, hb_s):
        step = pl.program_id(0)

        @pl.when(step == 0)
        def _():
            c_s[...] = spread_c(bc_ref[:, states:], states, False)

        strips = [
            h_ref[p, s * states : (s + 1) * states, :].astype(F32)
            for p in range(per_block)
            for s in range(share.strips)
        ]
        h_in = jnp.concatenate(strips, axis=1)
        for n in range(states):
            a_s[n] = jnp.broadcast_to(a_ref[n : n + 1, :] * (-LOG2E), (GROUP, block)).astype(BF16)
            hb_s[n] = jnp.broadcast_to(h_in[n : n + 1, :], (GROUP, block)).astype(BF16)

        def strip(c, _):
            lanes = pl.ds(pl.multiple_of(c * sub, sub), sub)
            for g in range(rows // GROUP):
                at = slice(g * GROUP, (g + 1) * GROUP)
                cum = cum_ref[at, lanes]
                parts = [jnp.exp2(cum * a_s[n, :, lanes]) * hb_s[n, :, lanes] for n in range(states)]
                fixed = jnp.dot(c_s[at, :], jnp.concatenate(parts, axis=0), preferred_element_type=F32)
                gate = gate_ref[at, lanes].astype(F32)
                out_ref[at, lanes] = ((y_ref[at, lanes] + fixed) * silu(gate)).astype(BF16)
            return 0

        lax.fori_loop(0, block // sub, strip, 0)

    return pl.pallas_call(
        body,
        grid=(count,),
        in_specs=[
            pl.BlockSpec((rows, block), lambda i: (0, i)),
            pl.BlockSpec((per_block, share.rows, share.lanes), lambda i: (i, 0, 0)),
            pl.BlockSpec((rows, block), lambda i: (0, i)),
            pl.BlockSpec((rows, block), lambda i: (0, i)),
            pl.BlockSpec((rows, 2 * states), lambda i: (0, 0)),
            pl.BlockSpec((states, block), lambda i: (0, i)),
        ],
        out_specs=pl.BlockSpec((rows, block), lambda i: (0, i)),
        out_shape=jax.ShapeDtypeStruct((rows, width), BF16),
        scratch_shapes=[
            pltpu.VMEM((rows, GROUP * states), BF16),
            pltpu.VMEM((states, GROUP, block), BF16),
            pltpu.VMEM((states, GROUP, block), BF16),
        ],
        name="final",
    )(cum, h_in, y, gate, bc, decay)


def local(x_in, gate_in, conv_weight, conv_bias, x_proj, dt_proj, dt_bias, decay_rates, skip_gain):
    rows, width = x_in.shape
    taps = conv_weight.shape[0]
    states = decay_rates.shape[0]
    parts = lax.axis_size(AXES)
    share = Share(width, parts, states)
    prior = lax.ppermute(x_in[rows - (taps - 1) :], AXES, [(p, p + 1) for p in range(parts - 1)])
    halo = jnp.pad(prior.astype(F32), ((8 - (taps - 1), 0), (0, 0)))
    y, cum, message, bc = front(
        x_in, halo, conv_weight, conv_bias[None], x_proj.T, dt_proj, dt_bias[None], decay_rates, skip_gain[None], share
    )
    got = lax.all_to_all(message, AXES, 0, 0, tiled=True)
    own = lax.dynamic_slice_in_dim(decay_rates, lax.axis_index(AXES) * share.width, share.width, 1)
    incoming = combine(got, own, share)
    h_in = lax.all_to_all(incoming, AXES, 0, 0, tiled=True)
    return final(cum, h_in, y, gate_in, bc, decay_rates, share)


def solution(mesh):
    split = P(AXES, None)
    return jax.shard_map(
        local,
        mesh=mesh,
        in_specs=(split, split, P(), P(), P(), P(), P(), P(), P()),
        out_specs=split,
        check_vma=False,
    )
```

```python
import jax
import jax.numpy as jnp
from jax import lax
from jax.experimental import pallas as pl
from jax.experimental.pallas import tpu as pltpu
from jax.sharding import PartitionSpec as P

AXES = ("outer", "inner")
LOG2E = 1.4426950408889634
DT_CEILING = 0.25
GROUP = 16
LANES = 128
HALO = 16
AHEAD = 2
VMEM_BYTES = 60 * 2**20
F32 = jnp.float32
BF16 = jnp.bfloat16


def silu(value):
    half = 0.5 * value
    return half + half * jnp.tanh(half)


def capped_softplus(value):
    z = jnp.exp(jnp.minimum(value, -1.0))
    w = 1.0 + z
    return jnp.minimum(jnp.log(w) + (z - (w - 1.0)), DT_CEILING)


def pick_block(width, limit):
    block = limit
    while width % block:
        block //= 2
    return block


def spread_c(cmat, states, by_token):
    rows = cmat.shape[0]
    wide = GROUP * states
    n = lax.broadcasted_iota(jnp.int32, (states, wide), 0)
    col = lax.broadcasted_iota(jnp.int32, (states, wide), 1)
    pick = col % states if by_token else col // GROUP
    select = jnp.where(n == pick, 1.0, 0.0).astype(BF16)
    spread = jnp.dot(cmat.astype(BF16), select, preferred_element_type=F32)
    t = lax.broadcasted_iota(jnp.int32, (rows, wide), 0) % GROUP
    col = lax.broadcasted_iota(jnp.int32, (rows, wide), 1)
    token = col // states if by_token else col % GROUP
    return jnp.where(t == token, spread, 0.0).astype(BF16)


class Share:
    def __init__(self, width, parts, states):
        self.width = width // parts
        self.lanes = min(self.width, LANES)
        self.strips = self.width // self.lanes
        self.states = states
        self.rows = states * self.strips
        self.message_rows = -(-(self.rows + 2 * self.strips) // 8) * 8


def front(x_in, halo, conv_weight, conv_bias, x_proj_t, dt_proj, dt_bias, decay, skip, share):
    rows, width = x_in.shape
    taps = conv_weight.shape[0]
    rank = dt_proj.shape[0]
    states = decay.shape[0]
    columns = x_proj_t.shape[0]
    block = pick_block(width, 1024)
    count = width // block
    per_block = block // share.width
    groups = rows // GROUP
    wide = pick_block(width, 1024)
    chunks = width // wide
    ratio = wide // block

    def body(x_hbm, halo_hbm, cw_hbm, cb_hbm, xp_hbm, dp_hbm, bias_hbm, a_hbm, skip_hbm,
             y_hbm, cum_hbm, msg_ref, bc_ref,
             x_s, xp_s, dp_s, u_s, y_s, cum_s, cw_ref, cb_ref, bias_ref, a_ref, skip_ref,
             halo_s, proj, low, hl, b_s, c_s, dt_s, v_s, h0_s, h1_s, add0_s, add1_s, rates, shift_s,
             x_sem, xp_sem, dp_sem, y_sem, cum_sem, small_sem):
        h_s = (h0_s, h1_s)
        add_s = (add0_s, add1_s)
        small = [
            pltpu.make_async_copy(source, target, small_sem.at[i])
            for i, (source, target) in enumerate(
                (
                    (halo_hbm, halo_s),
                    (cw_hbm, cw_ref),
                    (cb_hbm, cb_ref),
                    (a_hbm, a_ref),
                    (bias_hbm, bias_ref),
                    (skip_hbm, skip_ref),
                )
            )
        ]

        def at(j):
            return pl.ds(pl.multiple_of(j * block, block), block)

        def chunk(c):
            return pl.ds(pl.multiple_of(c * wide, wide), wide)

        def copies_in(c):
            return (
                pltpu.make_async_copy(x_hbm.at[:, chunk(c)], x_s.at[:rows, chunk(c)], x_sem.at[c]),
                pltpu.make_async_copy(xp_hbm.at[:, chunk(c)], xp_s.at[:, chunk(c)], xp_sem.at[c]),
            )

        def copy_dp(c):
            return pltpu.make_async_copy(dp_hbm.at[:, chunk(c)], dp_s.at[:, chunk(c)], dp_sem.at[c])

        def copies_out(c):
            return (
                pltpu.make_async_copy(y_s.at[:, chunk(c)], y_hbm.at[:, chunk(c)], y_sem.at[c]),
                pltpu.make_async_copy(cum_s.at[:, chunk(c)], cum_hbm.at[:, chunk(c)], cum_sem.at[c]),
            )

        for copy in small[:3]:
            copy.start()
        for c in range(min(AHEAD, chunks)):
            for copy in copies_in(c):
                copy.start()
        proj[...] = jnp.zeros_like(proj)

        line = lax.broadcasted_iota(jnp.int32, (rows, rows + HALO), 0)
        source = lax.broadcasted_iota(jnp.int32, (rows, rows + HALO), 1)
        for k in range(taps):
            want = line - (taps - 1 - k)
            want = jnp.where(want < 0, want + rows + taps - 1, want)
            shift_s[k * rows : (k + 1) * rows, :] = jnp.where(source == want, 1.0, 0.0).astype(BF16)
        x_s[rows:, :] = jnp.zeros((HALO, width), BF16)
        for copy in small[:3]:
            copy.wait()
        x_s[rows : rows + taps - 1, :] = halo_s[...]

        def head(j):
            lanes = at(j)
            moved = jnp.dot(shift_s[...], x_s[:, lanes], preferred_element_type=F32)
            conv = cb_ref[:, lanes]
            for k in range(taps):
                conv = conv + cw_ref[k : k + 1, lanes] * moved[k * rows : (k + 1) * rows]
            u = silu(conv).astype(BF16)
            u_s[:, lanes] = u
            proj[...] += lax.dot_general(u, xp_s[:, lanes], (((1,), (1,)), ((), ())), preferred_element_type=F32)

        def head_chunk(c, _):
            for copy in copies_in(c):
                copy.wait()

            @pl.when(c + AHEAD < chunks)
            def _():
                for copy in copies_in(c + AHEAD):
                    copy.start()

            @pl.when(c + AHEAD == chunks)
            def _():
                for copy in small[3:]:
                    copy.start()
                for d in range(chunks):
                    copy_dp(d).start()

            for r in range(ratio):
                head(c * ratio + r)
            return 0

        lax.fori_loop(0, chunks, head_chunk, 0)

        low[...] = proj[:, :rank].astype(BF16)
        bmat = proj[:, rank : rank + states]
        cmat = proj[:, rank + states : rank + 2 * states]
        bc_ref[...] = proj[:, rank:]
        c_s[...] = spread_c(cmat, states, True)
        high = bmat.astype(BF16).astype(F32)
        hl[...] = jnp.zeros_like(hl)
        hl[:, :states] = high
        hl[:, states : 2 * states] = bmat - high
        n = lax.broadcasted_iota(jnp.int32, (states, LANES), 0)
        lane = lax.broadcasted_iota(jnp.int32, (states, LANES), 1)
        keep = jnp.logical_or(lane == n, lane == n + states)
        ones = jnp.ones((LANES, LANES), BF16)
        token = lax.broadcasted_iota(jnp.int32, (GROUP * states, LANES), 1)
        own = lax.broadcasted_iota(jnp.int32, (GROUP * states, LANES), 0) // states

        def fill(g, _):
            base = pl.multiple_of(g * GROUP, GROUP)
            picked = [
                jnp.where(keep, jnp.broadcast_to(hl[pl.ds(base + i, 1), :], (states, LANES)), 0.0).astype(BF16)
                for i in range(GROUP)
            ]
            spread = jnp.dot(jnp.concatenate(picked, axis=0), ones, preferred_element_type=F32)
            b_s[g] = jnp.where(token == own, spread, 0.0)[:, :GROUP].astype(BF16)
            return 0

        lax.fori_loop(0, groups, fill, 0)

        row = lax.broadcasted_iota(jnp.int32, (rows, rows), 0)
        col = lax.broadcasted_iota(jnp.int32, (rows, rows), 1)
        tri = jnp.where(row >= col, 1.0, 0.0).astype(BF16)
        for copy in small[3:]:
            copy.wait()
        fill_rows = share.message_rows - share.rows - 2 * share.strips

        def tail(j, _):
            lanes = at(j)

            @pl.when(j % ratio == 0)
            def _():
                copy_dp(j // ratio).wait()

            raw = jnp.dot(low[...], dp_s[:, lanes], preferred_element_type=F32)
            dt = capped_softplus(raw + bias_ref[:, lanes])
            dt_s[...] = dt
            v_s[...] = (dt * u_s[:, lanes].astype(F32)).astype(BF16)
            cum = jnp.dot(tri, dt.astype(BF16), preferred_element_type=F32)
            cum_s[:, lanes] = cum.astype(BF16)
            total = cum[rows - 1 : rows]
            rates[...] = a_ref[:, lanes] * (-LOG2E)
            skip_row = skip_ref[:, lanes]

            def load(g):
                add_s[g % 2][...] = jnp.dot(
                    b_s[g], v_s[g * GROUP : (g + 1) * GROUP, :], preferred_element_type=F32
                )

            def scan_group(g, h):
                for i in range(GROUP):
                    t = g * GROUP + i
                    at_i = slice(i * states, (i + 1) * states)
                    dtb = jnp.broadcast_to(dt_s[t : t + 1, :], (states, block))
                    h = jnp.exp2(dtb * rates[...]) * h + add_s[g % 2][at_i, :]
                    h_s[g % 2][at_i, :] = h.astype(BF16)
                return h

            def emit(g):
                tokens = slice(g * GROUP, (g + 1) * GROUP)
                y = jnp.dot(c_s[tokens, :], h_s[g % 2][...], preferred_element_type=F32)
                y_s[tokens, lanes] = y + skip_row * u_s[tokens, lanes].astype(F32)

            h = jnp.zeros((states, block), F32)
            load(0)
            for g in range(groups):
                if g + 1 < groups:
                    load(g + 1)
                if g > 0:
                    emit(g - 1)
                h = scan_group(g, h)
            emit(groups - 1)

            @pl.when(j % ratio == ratio - 1)
            def _():
                for copy in copies_out(j // ratio):
                    copy.start()

            high = total.astype(BF16).astype(F32)
            rest = total - high
            for p in range(per_block):
                cuts = [
                    slice(p * share.width + s * share.lanes, p * share.width + (s + 1) * share.lanes)
                    for s in range(share.strips)
                ]
                pieces = [h[:, c] for c in cuts] + [high[:, c] for c in cuts] + [rest[:, c] for c in cuts]
                if fill_rows:
                    pieces.append(jnp.zeros((fill_rows, share.lanes), F32))
                msg_ref[j * per_block + p] = jnp.concatenate(pieces, axis=0).astype(BF16)
            return 0

        lax.fori_loop(0, count, tail, 0)
        for c in range(chunks):
            for copy in copies_out(c):
                copy.wait()

    whole = pl.BlockSpec(memory_space=pltpu.VMEM)
    held = pl.BlockSpec(memory_space=pltpu.HBM)
    return pl.pallas_call(
        body,
        in_specs=[held] * 9,
        out_specs=[held, held, whole, whole],
        out_shape=[
            jax.ShapeDtypeStruct((rows, width), F32),
            jax.ShapeDtypeStruct((rows, width), BF16),
            jax.ShapeDtypeStruct((width // share.width, share.message_rows, share.lanes), BF16),
            jax.ShapeDtypeStruct((rows, 2 * states), F32),
        ],
        scratch_shapes=[
            pltpu.VMEM((rows + HALO, width), BF16),
            pltpu.VMEM((columns, width), BF16),
            pltpu.VMEM((rank, width), BF16),
            pltpu.VMEM((rows, width), BF16),
            pltpu.VMEM((rows, width), F32),
            pltpu.VMEM((rows, width), BF16),
            pltpu.VMEM((taps, width), F32),
            pltpu.VMEM((1, width), F32),
            pltpu.VMEM((1, width), F32),
            pltpu.VMEM((states, width), F32),
            pltpu.VMEM((1, width), F32),
            pltpu.VMEM((taps - 1, width), BF16),
            pltpu.VMEM((rows, columns), F32),
            pltpu.VMEM((rows, rank), BF16),
            pltpu.VMEM((rows, LANES), F32),
            pltpu.VMEM((groups, GROUP * states, GROUP), BF16),
            pltpu.VMEM((rows, GROUP * states), BF16),
            pltpu.VMEM((rows, block), F32),
            pltpu.VMEM((rows, block), BF16),
            pltpu.VMEM((GROUP * states, block), BF16),
            pltpu.VMEM((GROUP * states, block), BF16),
            pltpu.VMEM((GROUP * states, block), F32),
            pltpu.VMEM((GROUP * states, block), F32),
            pltpu.VMEM((states, block), F32),
            pltpu.VMEM((taps * rows, rows + HALO), BF16),
        ]
        + [pltpu.SemaphoreType.DMA((chunks,))] * 5
        + [pltpu.SemaphoreType.DMA((6,))],
        compiler_params=pltpu.CompilerParams(vmem_limit_bytes=VMEM_BYTES),
        name="front",
    )(x_in, halo, conv_weight, conv_bias, x_proj_t, dt_proj, dt_bias, decay, skip)


def combine(message, decay, mine, share):
    parts = message.shape[0]
    states = share.states
    aligned = share.width % LANES == 0
    if not aligned:
        decay = lax.dynamic_slice_in_dim(decay, mine * share.width, share.width, 1)

    def body(mine_ref, msg_ref, a_hbm, h_ref, a_s, sem):
        source = a_hbm
        if aligned:
            source = a_hbm.at[:, pl.ds(pl.multiple_of(mine_ref[0] * share.width, LANES), share.width)]
        copy = pltpu.make_async_copy(source, a_s, sem.at[0])
        copy.start()
        copy.wait()
        rates = [a_s[:, s * share.lanes : (s + 1) * share.lanes] * (-LOG2E) for s in range(share.strips)]

        def one(p, carry):
            later = []
            for s, h in enumerate(carry):
                h_ref[p, s * states : (s + 1) * states, :] = h.astype(BF16)
                high = msg_ref[p, share.rows + s : share.rows + s + 1, :].astype(F32)
                at = share.rows + share.strips + s
                total = high + msg_ref[p, at : at + 1, :].astype(F32)
                add = msg_ref[p, s * states : (s + 1) * states, :].astype(F32)
                later.append(jnp.exp2(rates[s] * total) * h + add)
            return tuple(later)

        zero = jnp.zeros((states, share.lanes), F32)
        lax.fori_loop(0, parts, one, (zero,) * share.strips, unroll=8)

    whole = pl.BlockSpec(memory_space=pltpu.VMEM)
    return pl.pallas_call(
        body,
        in_specs=[pl.BlockSpec(memory_space=pltpu.SMEM), whole, pl.BlockSpec(memory_space=pltpu.HBM)],
        out_specs=whole,
        out_shape=jax.ShapeDtypeStruct((parts, share.rows, share.lanes), BF16),
        scratch_shapes=[pltpu.VMEM((states, share.width), F32), pltpu.SemaphoreType.DMA((1,))],
        name="combine",
    )(mine[None], message, decay)


def final(cum, h_in, y, gate, bc, decay, share):
    rows, width = cum.shape
    states = decay.shape[0]
    wide = pick_block(width, 1024)
    block = pick_block(wide, 256)
    count = width // block
    chunks = width // wide
    ratio = wide // block
    per_block = block // share.width

    def body(cum_hbm, h_ref, y_hbm, gate_hbm, bc_ref, a_hbm, out_hbm,
             cum_s, y_s, gate_s, out_s, a_ref, c_s, cum_sem, y_sem, gate_sem, out_sem, a_sem):
        def at(j):
            return pl.ds(pl.multiple_of(j * block, block), block)

        def chunk(c):
            return pl.ds(pl.multiple_of(c * wide, wide), wide)

        def copies_in(c):
            return (
                pltpu.make_async_copy(cum_hbm.at[:, chunk(c)], cum_s.at[:, chunk(c)], cum_sem.at[c]),
                pltpu.make_async_copy(y_hbm.at[:, chunk(c)], y_s.at[:, chunk(c)], y_sem.at[c]),
                pltpu.make_async_copy(gate_hbm.at[:, chunk(c)], gate_s.at[:, chunk(c)], gate_sem.at[c]),
            )

        def copy_out(c):
            return pltpu.make_async_copy(out_s.at[:, chunk(c)], out_hbm.at[:, chunk(c)], out_sem.at[c])

        copy_a = pltpu.make_async_copy(a_hbm, a_ref, a_sem.at[0])
        copy_a.start()
        for c in range(min(AHEAD, chunks)):
            for copy in copies_in(c):
                copy.start()
        c_s[...] = spread_c(bc_ref[:, states:], states, False)
        copy_a.wait()

        def strip(j, _):
            lanes = at(j)
            strips = [
                h_ref[j * per_block + p, s * states : (s + 1) * states, :].astype(F32)
                for p in range(per_block)
                for s in range(share.strips)
            ]
            h_in = jnp.concatenate(strips, axis=1)
            rates = a_ref[:, lanes] * (-LOG2E)
            a_n = [jnp.broadcast_to(rates[n : n + 1], (GROUP, block)).astype(BF16) for n in range(states)]
            h_n = [jnp.broadcast_to(h_in[n : n + 1], (GROUP, block)).astype(BF16) for n in range(states)]
            for g in range(rows // GROUP):
                tokens = slice(g * GROUP, (g + 1) * GROUP)
                cum = cum_s[tokens, lanes]
                parts = [jnp.exp2(cum * a_n[n]) * h_n[n] for n in range(states)]
                fixed = jnp.dot(c_s[tokens, :], jnp.concatenate(parts, axis=0), preferred_element_type=F32)
                gate = gate_s[tokens, lanes].astype(F32)
                out_s[tokens, lanes] = ((y_s[tokens, lanes] + fixed) * silu(gate)).astype(BF16)
            return 0

        def run_chunk(c, _):
            for copy in copies_in(c):
                copy.wait()

            @pl.when(c + AHEAD < chunks)
            def _():
                for copy in copies_in(c + AHEAD):
                    copy.start()

            lax.fori_loop(c * ratio, (c + 1) * ratio, strip, 0)
            copy_out(c).start()
            return 0

        lax.fori_loop(0, chunks, run_chunk, 0)
        for c in range(chunks):
            copy_out(c).wait()

    whole = pl.BlockSpec(memory_space=pltpu.VMEM)
    held = pl.BlockSpec(memory_space=pltpu.HBM)
    return pl.pallas_call(
        body,
        in_specs=[held, whole, held, held, whole, held],
        out_specs=held,
        out_shape=jax.ShapeDtypeStruct((rows, width), BF16),
        scratch_shapes=[
            pltpu.VMEM((rows, width), BF16),
            pltpu.VMEM((rows, width), F32),
            pltpu.VMEM((rows, width), BF16),
            pltpu.VMEM((rows, width), BF16),
            pltpu.VMEM((states, width), F32),
            pltpu.VMEM((rows, GROUP * states), BF16),
        ]
        + [pltpu.SemaphoreType.DMA((chunks,))] * 4
        + [pltpu.SemaphoreType.DMA((1,))],
        compiler_params=pltpu.CompilerParams(vmem_limit_bytes=VMEM_BYTES),
        name="final",
    )(cum, h_in, y, gate, bc, decay)


def local(x_in, gate_in, conv_weight, conv_bias, x_proj, dt_proj, dt_bias, decay_rates, skip_gain):
    rows, width = x_in.shape
    taps = conv_weight.shape[0]
    states = decay_rates.shape[0]
    parts = lax.axis_size(AXES)
    share = Share(width, parts, states)
    prior = lax.ppermute(x_in[rows - (taps - 1) :], AXES, [(p, p + 1) for p in range(parts - 1)])
    mine = lax.axis_index(AXES).astype(jnp.int32)
    y, cum, message, bc = front(
        x_in, prior, conv_weight, conv_bias[None], x_proj.T, dt_proj, dt_bias[None], decay_rates, skip_gain[None], share
    )
    got = lax.all_to_all(message, AXES, 0, 0, tiled=True)
    incoming = combine(got, decay_rates, mine, share)
    h_in = lax.all_to_all(incoming, AXES, 0, 0, tiled=True)
    return final(cum, h_in, y, gate_in, bc, decay_rates, share)


def solution(mesh):
    split = P(AXES, None)
    return jax.shard_map(
        local,
        mesh=mesh,
        in_specs=(split, split, P(), P(), P(), P(), P(), P(), P()),
        out_specs=split,
        check_vma=False,
    )
```

```python
import jax
import jax.numpy as jnp
from jax import lax
from jax.experimental import pallas as pl
from jax.experimental.pallas import tpu as pltpu
from jax.sharding import PartitionSpec as P

AXES = ("outer", "inner")
LOG2E = 1.4426950408889634
DT_CEILING = 0.25
GROUP = 16
LANES = 128
HALO = 16
AHEAD = 2
VMEM_BYTES = 60 * 2**20
F32 = jnp.float32
BF16 = jnp.bfloat16


def silu(value):
    half = 0.5 * value
    return half + half * jnp.tanh(half)


def capped_softplus(value):
    z = jnp.exp(jnp.minimum(value, -1.0))
    w = 1.0 + z
    return jnp.minimum(jnp.log(w) + (z - (w - 1.0)), DT_CEILING)


def pick_block(width, limit):
    block = limit
    while width % block:
        block //= 2
    return block


def spread_c(cmat, states, by_token):
    rows = cmat.shape[0]
    wide = GROUP * states
    n = lax.broadcasted_iota(jnp.int32, (states, wide), 0)
    col = lax.broadcasted_iota(jnp.int32, (states, wide), 1)
    pick = col % states if by_token else col // GROUP
    select = jnp.where(n == pick, 1.0, 0.0).astype(BF16)
    spread = jnp.dot(cmat.astype(BF16), select, preferred_element_type=F32)
    t = lax.broadcasted_iota(jnp.int32, (rows, wide), 0) % GROUP
    col = lax.broadcasted_iota(jnp.int32, (rows, wide), 1)
    token = col // states if by_token else col % GROUP
    return jnp.where(t == token, spread, 0.0).astype(BF16)


class Share:
    def __init__(self, width, parts, states):
        self.width = width // parts
        self.lanes = min(self.width, LANES)
        self.strips = self.width // self.lanes
        self.states = states
        self.rows = states * self.strips
        self.message_rows = -(-(self.rows + 2 * self.strips) // 8) * 8


def front(x_in, halo, conv_weight, conv_bias, x_proj_t, dt_proj, dt_bias, decay, skip, share):
    rows, width = x_in.shape
    taps = conv_weight.shape[0]
    rank = dt_proj.shape[0]
    states = decay.shape[0]
    columns = x_proj_t.shape[0]
    block = pick_block(width, 1024)
    count = width // block
    per_block = block // share.width
    groups = rows // GROUP
    wide = pick_block(width, 1024)
    chunks = width // wide
    ratio = wide // block

    def body(x_hbm, halo_hbm, cw_hbm, cb_hbm, xp_hbm, dp_hbm, bias_hbm, a_hbm, skip_hbm,
             y_hbm, cum_hbm, msg_ref, bc_ref,
             x_s, xp_s, dp_s, u_s, y_s, cum_s, cw_ref, cb_ref, bias_ref, a_ref, skip_ref,
             halo_s, proj, low, hl, b_s, c_s, dt_s, v_s, h0_s, h1_s, add0_s, add1_s, rates, shift_s,
             x_sem, xp_sem, dp_sem, y_sem, cum_sem, small_sem):
        h_s = (h0_s, h1_s)
        add_s = (add0_s, add1_s)
        small = [
            pltpu.make_async_copy(source, target, small_sem.at[i])
            for i, (source, target) in enumerate(
                (
                    (halo_hbm, halo_s),
                    (cw_hbm, cw_ref),
                    (cb_hbm, cb_ref),
                    (a_hbm, a_ref),
                    (bias_hbm, bias_ref),
                    (skip_hbm, skip_ref),
                )
            )
        ]

        def at(j):
            return pl.ds(pl.multiple_of(j * block, block), block)

        def chunk(c):
            return pl.ds(pl.multiple_of(c * wide, wide), wide)

        def copies_in(c):
            return (
                pltpu.make_async_copy(x_hbm.at[:, chunk(c)], x_s.at[:rows, chunk(c)], x_sem.at[c]),
                pltpu.make_async_copy(xp_hbm.at[:, chunk(c)], xp_s.at[:, chunk(c)], xp_sem.at[c]),
            )

        def copy_dp(c):
            return pltpu.make_async_copy(dp_hbm.at[:, chunk(c)], dp_s.at[:, chunk(c)], dp_sem.at[c])

        def copies_out(c):
            return (
                pltpu.make_async_copy(y_s.at[:, chunk(c)], y_hbm.at[:, chunk(c)], y_sem.at[c]),
                pltpu.make_async_copy(cum_s.at[:, chunk(c)], cum_hbm.at[:, chunk(c)], cum_sem.at[c]),
            )

        for copy in small[:3]:
            copy.start()
        for c in range(min(AHEAD, chunks)):
            for copy in copies_in(c):
                copy.start()
        proj[...] = jnp.zeros_like(proj)

        line = lax.broadcasted_iota(jnp.int32, (rows, rows + HALO), 0)
        source = lax.broadcasted_iota(jnp.int32, (rows, rows + HALO), 1)
        for k in range(taps):
            want = line - (taps - 1 - k)
            want = jnp.where(want < 0, want + rows + taps - 1, want)
            shift_s[k * rows : (k + 1) * rows, :] = jnp.where(source == want, 1.0, 0.0).astype(BF16)
        x_s[rows:, :] = jnp.zeros((HALO, width), BF16)
        for copy in small[:3]:
            copy.wait()
        x_s[rows : rows + taps - 1, :] = halo_s[...]

        def head(j):
            lanes = at(j)
            moved = jnp.dot(shift_s[...], x_s[:, lanes], preferred_element_type=F32)
            conv = cb_ref[:, lanes]
            for k in range(taps):
                conv = conv + cw_ref[k : k + 1, lanes] * moved[k * rows : (k + 1) * rows]
            u = silu(conv).astype(BF16)
            u_s[:, lanes] = u
            proj[...] += lax.dot_general(u, xp_s[:, lanes], (((1,), (1,)), ((), ())), preferred_element_type=F32)

        def head_chunk(c, _):
            for copy in copies_in(c):
                copy.wait()

            @pl.when(c + AHEAD < chunks)
            def _():
                for copy in copies_in(c + AHEAD):
                    copy.start()

            @pl.when(c + AHEAD == chunks)
            def _():
                for copy in small[3:]:
                    copy.start()
                for d in range(chunks):
                    copy_dp(d).start()

            for r in range(ratio):
                head(c * ratio + r)
            return 0

        lax.fori_loop(0, chunks, head_chunk, 0)

        low[...] = proj[:, :rank].astype(BF16)
        bmat = proj[:, rank : rank + states]
        cmat = proj[:, rank + states : rank + 2 * states]
        bc_ref[...] = proj[:, rank:]
        c_s[...] = spread_c(cmat, states, True)
        high = bmat.astype(BF16).astype(F32)
        hl[...] = jnp.zeros_like(hl)
        hl[:, :states] = high
        hl[:, states : 2 * states] = bmat - high
        n = lax.broadcasted_iota(jnp.int32, (states, LANES), 0)
        lane = lax.broadcasted_iota(jnp.int32, (states, LANES), 1)
        keep = jnp.logical_or(lane == n, lane == n + states)
        ones = jnp.ones((LANES, LANES), BF16)
        token = lax.broadcasted_iota(jnp.int32, (GROUP * states, LANES), 1)
        own = lax.broadcasted_iota(jnp.int32, (GROUP * states, LANES), 0) // states

        def fill(g, _):
            base = pl.multiple_of(g * GROUP, GROUP)
            picked = [
                jnp.where(keep, jnp.broadcast_to(hl[pl.ds(base + i, 1), :], (states, LANES)), 0.0).astype(BF16)
                for i in range(GROUP)
            ]
            spread = jnp.dot(jnp.concatenate(picked, axis=0), ones, preferred_element_type=F32)
            b_s[g] = jnp.where(token == own, spread, 0.0)[:, :GROUP].astype(BF16)
            return 0

        lax.fori_loop(0, groups, fill, 0)

        row = lax.broadcasted_iota(jnp.int32, (rows, rows), 0)
        col = lax.broadcasted_iota(jnp.int32, (rows, rows), 1)
        tri = jnp.where(row >= col, 1.0, 0.0).astype(BF16)
        for copy in small[3:]:
            copy.wait()
        fill_rows = share.message_rows - share.rows - 2 * share.strips

        def tail(j, _):
            lanes = at(j)

            @pl.when(j % ratio == 0)
            def _():
                copy_dp(j // ratio).wait()

            raw = jnp.dot(low[...], dp_s[:, lanes], preferred_element_type=F32)
            dt = capped_softplus(raw + bias_ref[:, lanes])
            dt_s[...] = dt
            v_s[...] = (dt * u_s[:, lanes].astype(F32)).astype(BF16)
            cum = jnp.dot(tri, dt.astype(BF16), preferred_element_type=F32)
            cum_s[:, lanes] = cum.astype(BF16)
            total = cum[rows - 1 : rows]
            rates[...] = a_ref[:, lanes] * (-LOG2E)
            skip_row = skip_ref[:, lanes]

            def load(g):
                add_s[g % 2][...] = jnp.dot(
                    b_s[g], v_s[g * GROUP : (g + 1) * GROUP, :], preferred_element_type=F32
                )

            def scan_group(g, h):
                for i in range(GROUP):
                    t = g * GROUP + i
                    at_i = slice(i * states, (i + 1) * states)
                    dtb = jnp.broadcast_to(dt_s[t : t + 1, :], (states, block))
                    h = jnp.exp2(dtb * rates[...]) * h + add_s[g % 2][at_i, :]
                    h_s[g % 2][at_i, :] = h.astype(BF16)
                return h

            def emit(g):
                tokens = slice(g * GROUP, (g + 1) * GROUP)
                y = jnp.dot(c_s[tokens, :], h_s[g % 2][...], preferred_element_type=F32)
                y_s[tokens, lanes] = y + skip_row * u_s[tokens, lanes].astype(F32)

            h = jnp.zeros((states, block), F32)
            load(0)
            for g in range(groups):
                if g + 1 < groups:
                    load(g + 1)
                if g > 0:
                    emit(g - 1)
                h = scan_group(g, h)
            emit(groups - 1)

            @pl.when(j % ratio == ratio - 1)
            def _():
                for copy in copies_out(j // ratio):
                    copy.start()

            high = total.astype(BF16).astype(F32)
            rest = total - high
            for p in range(per_block):
                cuts = [
                    slice(p * share.width + s * share.lanes, p * share.width + (s + 1) * share.lanes)
                    for s in range(share.strips)
                ]
                pieces = [h[:, c] for c in cuts] + [high[:, c] for c in cuts] + [rest[:, c] for c in cuts]
                if fill_rows:
                    pieces.append(jnp.zeros((fill_rows, share.lanes), F32))
                msg_ref[j * per_block + p] = jnp.concatenate(pieces, axis=0).astype(BF16)
            return 0

        lax.fori_loop(0, count, tail, 0)
        for c in range(chunks):
            for copy in copies_out(c):
                copy.wait()

    whole = pl.BlockSpec(memory_space=pltpu.VMEM)
    held = pl.BlockSpec(memory_space=pltpu.HBM)
    return pl.pallas_call(
        body,
        in_specs=[held] * 9,
        out_specs=[held, held, whole, whole],
        out_shape=[
            jax.ShapeDtypeStruct((rows, width), F32),
            jax.ShapeDtypeStruct((rows, width), BF16),
            jax.ShapeDtypeStruct((width // share.width, share.message_rows, share.lanes), BF16),
            jax.ShapeDtypeStruct((rows, 2 * states), F32),
        ],
        scratch_shapes=[
            pltpu.VMEM((rows + HALO, width), BF16),
            pltpu.VMEM((columns, width), BF16),
            pltpu.VMEM((rank, width), BF16),
            pltpu.VMEM((rows, width), BF16),
            pltpu.VMEM((rows, width), F32),
            pltpu.VMEM((rows, width), BF16),
            pltpu.VMEM((taps, width), F32),
            pltpu.VMEM((1, width), F32),
            pltpu.VMEM((1, width), F32),
            pltpu.VMEM((states, width), F32),
            pltpu.VMEM((1, width), F32),
            pltpu.VMEM((taps - 1, width), BF16),
            pltpu.VMEM((rows, columns), F32),
            pltpu.VMEM((rows, rank), BF16),
            pltpu.VMEM((rows, LANES), F32),
            pltpu.VMEM((groups, GROUP * states, GROUP), BF16),
            pltpu.VMEM((rows, GROUP * states), BF16),
            pltpu.VMEM((rows, block), F32),
            pltpu.VMEM((rows, block), BF16),
            pltpu.VMEM((GROUP * states, block), BF16),
            pltpu.VMEM((GROUP * states, block), BF16),
            pltpu.VMEM((GROUP * states, block), F32),
            pltpu.VMEM((GROUP * states, block), F32),
            pltpu.VMEM((states, block), F32),
            pltpu.VMEM((taps * rows, rows + HALO), BF16),
        ]
        + [pltpu.SemaphoreType.DMA((chunks,))] * 5
        + [pltpu.SemaphoreType.DMA((6,))],
        compiler_params=pltpu.CompilerParams(vmem_limit_bytes=VMEM_BYTES),
        name="front",
    )(x_in, halo, conv_weight, conv_bias, x_proj_t, dt_proj, dt_bias, decay, skip)


def combine(message, decay, mine, share):
    parts = message.shape[0]
    states = share.states
    aligned = share.width % LANES == 0
    if not aligned:
        decay = lax.dynamic_slice_in_dim(decay, mine * share.width, share.width, 1)

    def body(mine_ref, msg_ref, a_hbm, h_ref, a_s, sem):
        source = a_hbm
        if aligned:
            source = a_hbm.at[:, pl.ds(pl.multiple_of(mine_ref[0] * share.width, LANES), share.width)]
        copy = pltpu.make_async_copy(source, a_s, sem.at[0])
        copy.start()
        copy.wait()
        rates = [a_s[:, s * share.lanes : (s + 1) * share.lanes] * (-LOG2E) for s in range(share.strips)]

        def one(p, carry):
            later = []
            for s, h in enumerate(carry):
                h_ref[p, s * states : (s + 1) * states, :] = h.astype(BF16)
                high = msg_ref[p, share.rows + s : share.rows + s + 1, :].astype(F32)
                at = share.rows + share.strips + s
                total = high + msg_ref[p, at : at + 1, :].astype(F32)
                add = msg_ref[p, s * states : (s + 1) * states, :].astype(F32)
                later.append(jnp.exp2(rates[s] * total) * h + add)
            return tuple(later)

        zero = jnp.zeros((states, share.lanes), F32)
        lax.fori_loop(0, parts, one, (zero,) * share.strips, unroll=8)

    whole = pl.BlockSpec(memory_space=pltpu.VMEM)
    return pl.pallas_call(
        body,
        in_specs=[pl.BlockSpec(memory_space=pltpu.SMEM), whole, pl.BlockSpec(memory_space=pltpu.HBM)],
        out_specs=whole,
        out_shape=jax.ShapeDtypeStruct((parts, share.rows, share.lanes), BF16),
        scratch_shapes=[pltpu.VMEM((states, share.width), F32), pltpu.SemaphoreType.DMA((1,))],
        compiler_params=pltpu.CompilerParams(vmem_limit_bytes=8 * 2**20),
        name="combine",
    )(mine[None], message, decay)


def final(cum, h_in, y, gate, bc, decay, share):
    rows, width = cum.shape
    states = decay.shape[0]
    wide = pick_block(width, 1024)
    block = pick_block(wide, 256)
    count = width // block
    chunks = width // wide
    ratio = wide // block
    per_block = block // share.width

    def body(cum_hbm, h_ref, y_hbm, gate_hbm, bc_ref, a_hbm, out_hbm,
             cum_s, y_s, gate_s, out_s, a_ref, c_s, cum_sem, y_sem, gate_sem, out_sem, a_sem):
        def at(j):
            return pl.ds(pl.multiple_of(j * block, block), block)

        def chunk(c):
            return pl.ds(pl.multiple_of(c * wide, wide), wide)

        def copies_in(c):
            return (
                pltpu.make_async_copy(cum_hbm.at[:, chunk(c)], cum_s.at[:, chunk(c)], cum_sem.at[c]),
                pltpu.make_async_copy(y_hbm.at[:, chunk(c)], y_s.at[:, chunk(c)], y_sem.at[c]),
                pltpu.make_async_copy(gate_hbm.at[:, chunk(c)], gate_s.at[:, chunk(c)], gate_sem.at[c]),
            )

        def copy_out(c):
            return pltpu.make_async_copy(out_s.at[:, chunk(c)], out_hbm.at[:, chunk(c)], out_sem.at[c])

        copy_a = pltpu.make_async_copy(a_hbm, a_ref, a_sem.at[0])
        copy_a.start()
        for c in range(min(AHEAD, chunks)):
            for copy in copies_in(c):
                copy.start()
        c_s[...] = spread_c(bc_ref[:, states:], states, False)
        copy_a.wait()

        def strip(j, _):
            lanes = at(j)
            strips = [
                h_ref[j * per_block + p, s * states : (s + 1) * states, :].astype(F32)
                for p in range(per_block)
                for s in range(share.strips)
            ]
            h_in = jnp.concatenate(strips, axis=1)
            rates = a_ref[:, lanes] * (-LOG2E)
            a_n = [jnp.broadcast_to(rates[n : n + 1], (GROUP, block)).astype(BF16) for n in range(states)]
            h_n = [jnp.broadcast_to(h_in[n : n + 1], (GROUP, block)).astype(BF16) for n in range(states)]
            for g in range(rows // GROUP):
                tokens = slice(g * GROUP, (g + 1) * GROUP)
                cum = cum_s[tokens, lanes]
                parts = [jnp.exp2(cum * a_n[n]) * h_n[n] for n in range(states)]
                fixed = jnp.dot(c_s[tokens, :], jnp.concatenate(parts, axis=0), preferred_element_type=F32)
                gate = gate_s[tokens, lanes].astype(F32)
                out_s[tokens, lanes] = ((y_s[tokens, lanes] + fixed) * silu(gate)).astype(BF16)
            return 0

        def run_chunk(c, _):
            for copy in copies_in(c):
                copy.wait()

            @pl.when(c + AHEAD < chunks)
            def _():
                for copy in copies_in(c + AHEAD):
                    copy.start()

            lax.fori_loop(c * ratio, (c + 1) * ratio, strip, 0)
            copy_out(c).start()
            return 0

        lax.fori_loop(0, chunks, run_chunk, 0)
        for c in range(chunks):
            copy_out(c).wait()

    whole = pl.BlockSpec(memory_space=pltpu.VMEM)
    held = pl.BlockSpec(memory_space=pltpu.HBM)
    return pl.pallas_call(
        body,
        in_specs=[held, whole, held, held, whole, held],
        out_specs=held,
        out_shape=jax.ShapeDtypeStruct((rows, width), BF16),
        scratch_shapes=[
            pltpu.VMEM((rows, width), BF16),
            pltpu.VMEM((rows, width), F32),
            pltpu.VMEM((rows, width), BF16),
            pltpu.VMEM((rows, width), BF16),
            pltpu.VMEM((states, width), F32),
            pltpu.VMEM((rows, GROUP * states), BF16),
        ]
        + [pltpu.SemaphoreType.DMA((chunks,))] * 4
        + [pltpu.SemaphoreType.DMA((1,))],
        compiler_params=pltpu.CompilerParams(vmem_limit_bytes=VMEM_BYTES),
        name="final",
    )(cum, h_in, y, gate, bc, decay)


def local(x_in, gate_in, conv_weight, conv_bias, x_proj, dt_proj, dt_bias, decay_rates, skip_gain):
    rows, width = x_in.shape
    taps = conv_weight.shape[0]
    states = decay_rates.shape[0]
    parts = lax.axis_size(AXES)
    share = Share(width, parts, states)
    prior = lax.ppermute(x_in[rows - (taps - 1) :], AXES, [(p, p + 1) for p in range(parts - 1)])
    mine = lax.axis_index(AXES).astype(jnp.int32)
    y, cum, message, bc = front(
        x_in, prior, conv_weight, conv_bias[None], x_proj.T, dt_proj, dt_bias[None], decay_rates, skip_gain[None], share
    )
    got = lax.all_to_all(message, AXES, 0, 0, tiled=True)
    incoming = combine(got, decay_rates, mine, share)
    h_in = lax.all_to_all(incoming, AXES, 0, 0, tiled=True)
    return final(cum, h_in, y, gate_in, bc, decay_rates, share)


def solution(mesh):
    split = P(AXES, None)
    return jax.shard_map(
        local,
        mesh=mesh,
        in_specs=(split, split, P(), P(), P(), P(), P(), P(), P()),
        out_specs=split,
        check_vma=False,
    )
```

```python
import jax
import jax.numpy as jnp
from jax import lax
from jax.experimental import pallas as pl
from jax.experimental.pallas import tpu as pltpu
from jax.sharding import PartitionSpec as P

AXES = ("outer", "inner")
LOG2E = 1.4426950408889634
DT_CEILING = 0.25
GROUP = 16
LANES = 128
HALO = 16
AHEAD = 2
VMEM_BYTES = 60 * 2**20
F32 = jnp.float32
BF16 = jnp.bfloat16


def silu(value):
    half = 0.5 * value
    return half + half * jnp.tanh(half)


def capped_softplus(value):
    z = jnp.exp(jnp.minimum(value, -1.0))
    w = 1.0 + z
    return jnp.minimum(jnp.log(w) + (z - (w - 1.0)), DT_CEILING)


def pick_block(width, limit):
    block = limit
    while width % block:
        block //= 2
    return block


def spread_c(cmat, states, by_token):
    rows = cmat.shape[0]
    wide = GROUP * states
    n = lax.broadcasted_iota(jnp.int32, (states, wide), 0)
    col = lax.broadcasted_iota(jnp.int32, (states, wide), 1)
    pick = col % states if by_token else col // GROUP
    select = jnp.where(n == pick, 1.0, 0.0).astype(BF16)
    spread = jnp.dot(cmat.astype(BF16), select, preferred_element_type=F32)
    t = lax.broadcasted_iota(jnp.int32, (rows, wide), 0) % GROUP
    col = lax.broadcasted_iota(jnp.int32, (rows, wide), 1)
    token = col // states if by_token else col % GROUP
    return jnp.where(t == token, spread, 0.0).astype(BF16)


class Share:
    def __init__(self, width, parts, states):
        self.width = width // parts
        self.lanes = min(self.width, LANES)
        self.strips = self.width // self.lanes
        self.states = states
        self.rows = states * self.strips
        self.message_rows = -(-(self.rows + 2 * self.strips) // 8) * 8


def front(x_in, halo, conv_weight, conv_bias, x_proj_t, dt_proj, dt_bias, decay, skip, share):
    rows, width = x_in.shape
    taps = conv_weight.shape[0]
    rank = dt_proj.shape[0]
    states = decay.shape[0]
    columns = x_proj_t.shape[0]
    block = pick_block(width, 2048)
    count = width // block
    per_block = block // share.width
    groups = rows // GROUP
    wide = pick_block(width, 2048)
    chunks = width // wide
    ratio = wide // block

    def body(x_hbm, halo_hbm, cw_hbm, cb_hbm, xp_hbm, dp_hbm, bias_hbm, a_hbm, skip_hbm,
             y_hbm, cum_hbm, msg_ref, bc_ref,
             x_s, xp_s, dp_s, u_s, y_s, cum_s, cw_ref, cb_ref, bias_ref, a_ref, skip_ref,
             halo_s, proj, low, hl, b_s, c_s, dt_s, v_s, h0_s, h1_s, add0_s, add1_s, rates, shift_s,
             x_sem, xp_sem, dp_sem, y_sem, cum_sem, small_sem):
        h_s = (h0_s, h1_s)
        add_s = (add0_s, add1_s)
        small = [
            pltpu.make_async_copy(source, target, small_sem.at[i])
            for i, (source, target) in enumerate(
                (
                    (halo_hbm, halo_s),
                    (cw_hbm, cw_ref),
                    (cb_hbm, cb_ref),
                    (a_hbm, a_ref),
                    (bias_hbm, bias_ref),
                    (skip_hbm, skip_ref),
                )
            )
        ]

        def at(j):
            return pl.ds(pl.multiple_of(j * block, block), block)

        def chunk(c):
            return pl.ds(pl.multiple_of(c * wide, wide), wide)

        def copies_in(c):
            return (
                pltpu.make_async_copy(x_hbm.at[:, chunk(c)], x_s.at[:rows, chunk(c)], x_sem.at[c]),
                pltpu.make_async_copy(xp_hbm.at[:, chunk(c)], xp_s.at[:, chunk(c)], xp_sem.at[c]),
            )

        def copy_dp(c):
            return pltpu.make_async_copy(dp_hbm.at[:, chunk(c)], dp_s.at[:, chunk(c)], dp_sem.at[c])

        def copies_out(c):
            return (
                pltpu.make_async_copy(y_s.at[:, chunk(c)], y_hbm.at[:, chunk(c)], y_sem.at[c]),
                pltpu.make_async_copy(cum_s.at[:, chunk(c)], cum_hbm.at[:, chunk(c)], cum_sem.at[c]),
            )

        for copy in small[:3]:
            copy.start()
        for c in range(min(AHEAD, chunks)):
            for copy in copies_in(c):
                copy.start()
        proj[...] = jnp.zeros_like(proj)

        line = lax.broadcasted_iota(jnp.int32, (rows, rows + HALO), 0)
        source = lax.broadcasted_iota(jnp.int32, (rows, rows + HALO), 1)
        for k in range(taps):
            want = line - (taps - 1 - k)
            want = jnp.where(want < 0, want + rows + taps - 1, want)
            shift_s[k * rows : (k + 1) * rows, :] = jnp.where(source == want, 1.0, 0.0).astype(BF16)
        x_s[rows:, :] = jnp.zeros((HALO, width), BF16)
        for copy in small[:3]:
            copy.wait()
        x_s[rows : rows + taps - 1, :] = halo_s[...]

        def head(j):
            lanes = at(j)
            moved = jnp.dot(shift_s[...], x_s[:, lanes], preferred_element_type=F32)
            conv = cb_ref[:, lanes]
            for k in range(taps):
                conv = conv + cw_ref[k : k + 1, lanes] * moved[k * rows : (k + 1) * rows]
            u = silu(conv).astype(BF16)
            u_s[:, lanes] = u
            proj[...] += lax.dot_general(u, xp_s[:, lanes], (((1,), (1,)), ((), ())), preferred_element_type=F32)

        def head_chunk(c, _):
            for copy in copies_in(c):
                copy.wait()

            @pl.when(c + AHEAD < chunks)
            def _():
                for copy in copies_in(c + AHEAD):
                    copy.start()

            @pl.when(c + AHEAD == chunks)
            def _():
                for copy in small[3:]:
                    copy.start()
                for d in range(chunks):
                    copy_dp(d).start()

            for r in range(ratio):
                head(c * ratio + r)
            return 0

        lax.fori_loop(0, chunks, head_chunk, 0)

        low[...] = proj[:, :rank].astype(BF16)
        bmat = proj[:, rank : rank + states]
        cmat = proj[:, rank + states : rank + 2 * states]
        bc_ref[...] = proj[:, rank:]
        c_s[...] = spread_c(cmat, states, True)
        high = bmat.astype(BF16).astype(F32)
        hl[...] = jnp.zeros_like(hl)
        hl[:, :states] = high
        hl[:, states : 2 * states] = bmat - high
        n = lax.broadcasted_iota(jnp.int32, (states, LANES), 0)
        lane = lax.broadcasted_iota(jnp.int32, (states, LANES), 1)
        keep = jnp.logical_or(lane == n, lane == n + states)
        ones = jnp.ones((LANES, LANES), BF16)
        token = lax.broadcasted_iota(jnp.int32, (GROUP * states, LANES), 1)
        own = lax.broadcasted_iota(jnp.int32, (GROUP * states, LANES), 0) // states

        def fill(g, _):
            base = pl.multiple_of(g * GROUP, GROUP)
            picked = [
                jnp.where(keep, jnp.broadcast_to(hl[pl.ds(base + i, 1), :], (states, LANES)), 0.0).astype(BF16)
                for i in range(GROUP)
            ]
            spread = jnp.dot(jnp.concatenate(picked, axis=0), ones, preferred_element_type=F32)
            b_s[g] = jnp.where(token == own, spread, 0.0)[:, :GROUP].astype(BF16)
            return 0

        lax.fori_loop(0, groups, fill, 0)

        row = lax.broadcasted_iota(jnp.int32, (rows, rows), 0)
        col = lax.broadcasted_iota(jnp.int32, (rows, rows), 1)
        tri = jnp.where(row >= col, 1.0, 0.0).astype(BF16)
        for copy in small[3:]:
            copy.wait()
        fill_rows = share.message_rows - share.rows - 2 * share.strips

        def tail(j, _):
            lanes = at(j)

            @pl.when(j % ratio == 0)
            def _():
                copy_dp(j // ratio).wait()

            raw = jnp.dot(low[...], dp_s[:, lanes], preferred_element_type=F32)
            dt = capped_softplus(raw + bias_ref[:, lanes])
            dt_s[...] = dt
            v_s[...] = (dt * u_s[:, lanes].astype(F32)).astype(BF16)
            cum = jnp.dot(tri, dt.astype(BF16), preferred_element_type=F32)
            cum_s[:, lanes] = cum.astype(BF16)
            total = cum[rows - 1 : rows]
            rates[...] = a_ref[:, lanes] * (-LOG2E)
            skip_row = skip_ref[:, lanes]

            def load(g):
                add_s[g % 2][...] = jnp.dot(
                    b_s[g], v_s[g * GROUP : (g + 1) * GROUP, :], preferred_element_type=F32
                )

            def scan_group(g, h):
                for i in range(GROUP):
                    t = g * GROUP + i
                    at_i = slice(i * states, (i + 1) * states)
                    dtb = jnp.broadcast_to(dt_s[t : t + 1, :], (states, block))
                    h = jnp.exp2(dtb * rates[...]) * h + add_s[g % 2][at_i, :]
                    h_s[g % 2][at_i, :] = h.astype(BF16)
                return h

            def emit(g):
                tokens = slice(g * GROUP, (g + 1) * GROUP)
                y = jnp.dot(c_s[tokens, :], h_s[g % 2][...], preferred_element_type=F32)
                y_s[tokens, lanes] = y + skip_row * u_s[tokens, lanes].astype(F32)

            h = jnp.zeros((states, block), F32)
            load(0)
            for g in range(groups):
                if g + 1 < groups:
                    load(g + 1)
                if g > 0:
                    emit(g - 1)
                h = scan_group(g, h)
            emit(groups - 1)

            @pl.when(j % ratio == ratio - 1)
            def _():
                for copy in copies_out(j // ratio):
                    copy.start()

            high = total.astype(BF16).astype(F32)
            rest = total - high
            for p in range(per_block):
                cuts = [
                    slice(p * share.width + s * share.lanes, p * share.width + (s + 1) * share.lanes)
                    for s in range(share.strips)
                ]
                pieces = [h[:, c] for c in cuts] + [high[:, c] for c in cuts] + [rest[:, c] for c in cuts]
                if fill_rows:
                    pieces.append(jnp.zeros((fill_rows, share.lanes), F32))
                msg_ref[j * per_block + p] = jnp.concatenate(pieces, axis=0).astype(BF16)
            return 0

        lax.fori_loop(0, count, tail, 0)
        for c in range(chunks):
            for copy in copies_out(c):
                copy.wait()

    whole = pl.BlockSpec(memory_space=pltpu.VMEM)
    held = pl.BlockSpec(memory_space=pltpu.HBM)
    return pl.pallas_call(
        body,
        in_specs=[held] * 9,
        out_specs=[held, held, whole, whole],
        out_shape=[
            jax.ShapeDtypeStruct((rows, width), F32),
            jax.ShapeDtypeStruct((rows, width), BF16),
            jax.ShapeDtypeStruct((width // share.width, share.message_rows, share.lanes), BF16),
            jax.ShapeDtypeStruct((rows, 2 * states), F32),
        ],
        scratch_shapes=[
            pltpu.VMEM((rows + HALO, width), BF16),
            pltpu.VMEM((columns, width), BF16),
            pltpu.VMEM((rank, width), BF16),
            pltpu.VMEM((rows, width), BF16),
            pltpu.VMEM((rows, width), F32),
            pltpu.VMEM((rows, width), BF16),
            pltpu.VMEM((taps, width), F32),
            pltpu.VMEM((1, width), F32),
            pltpu.VMEM((1, width), F32),
            pltpu.VMEM((states, width), F32),
            pltpu.VMEM((1, width), F32),
            pltpu.VMEM((taps - 1, width), BF16),
            pltpu.VMEM((rows, columns), F32),
            pltpu.VMEM((rows, rank), BF16),
            pltpu.VMEM((rows, LANES), F32),
            pltpu.VMEM((groups, GROUP * states, GROUP), BF16),
            pltpu.VMEM((rows, GROUP * states), BF16),
            pltpu.VMEM((rows, block), F32),
            pltpu.VMEM((rows, block), BF16),
            pltpu.VMEM((GROUP * states, block), BF16),
            pltpu.VMEM((GROUP * states, block), BF16),
            pltpu.VMEM((GROUP * states, block), F32),
            pltpu.VMEM((GROUP * states, block), F32),
            pltpu.VMEM((states, block), F32),
            pltpu.VMEM((taps * rows, rows + HALO), BF16),
        ]
        + [pltpu.SemaphoreType.DMA((chunks,))] * 5
        + [pltpu.SemaphoreType.DMA((6,))],
        compiler_params=pltpu.CompilerParams(vmem_limit_bytes=VMEM_BYTES),
        name="front",
    )(x_in, halo, conv_weight, conv_bias, x_proj_t, dt_proj, dt_bias, decay, skip)


def combine(message, decay, mine, share):
    parts = message.shape[0]
    states = share.states
    aligned = share.width % LANES == 0
    if not aligned:
        decay = lax.dynamic_slice_in_dim(decay, mine * share.width, share.width, 1)

    def body(mine_ref, msg_ref, a_hbm, h_ref, a_s, sem):
        source = a_hbm
        if aligned:
            source = a_hbm.at[:, pl.ds(pl.multiple_of(mine_ref[0] * share.width, LANES), share.width)]
        copy = pltpu.make_async_copy(source, a_s, sem.at[0])
        copy.start()
        copy.wait()
        rates = [a_s[:, s * share.lanes : (s + 1) * share.lanes] * (-LOG2E) for s in range(share.strips)]

        def one(p, carry):
            later = []
            for s, h in enumerate(carry):
                h_ref[p, s * states : (s + 1) * states, :] = h.astype(BF16)
                high = msg_ref[p, share.rows + s : share.rows + s + 1, :].astype(F32)
                at = share.rows + share.strips + s
                total = high + msg_ref[p, at : at + 1, :].astype(F32)
                add = msg_ref[p, s * states : (s + 1) * states, :].astype(F32)
                later.append(jnp.exp2(rates[s] * total) * h + add)
            return tuple(later)

        zero = jnp.zeros((states, share.lanes), F32)
        lax.fori_loop(0, parts, one, (zero,) * share.strips, unroll=8)

    whole = pl.BlockSpec(memory_space=pltpu.VMEM)
    return pl.pallas_call(
        body,
        in_specs=[pl.BlockSpec(memory_space=pltpu.SMEM), whole, pl.BlockSpec(memory_space=pltpu.HBM)],
        out_specs=whole,
        out_shape=jax.ShapeDtypeStruct((parts, share.rows, share.lanes), BF16),
        scratch_shapes=[pltpu.VMEM((states, share.width), F32), pltpu.SemaphoreType.DMA((1,))],
        compiler_params=pltpu.CompilerParams(vmem_limit_bytes=8 * 2**20),
        name="combine",
    )(mine[None], message, decay)


def final(cum, h_in, y, gate, bc, decay, share):
    rows, width = cum.shape
    states = decay.shape[0]
    wide = pick_block(width, 2048)
    block = wide
    count = width // block
    chunks = width // wide
    ratio = wide // block
    per_block = block // share.width

    def body(cum_hbm, h_ref, y_hbm, gate_hbm, bc_ref, a_hbm, out_hbm,
             cum_s, y_s, gate_s, out_s, a_ref, c_s, cum_sem, y_sem, gate_sem, out_sem, a_sem):
        def at(j):
            return pl.ds(pl.multiple_of(j * block, block), block)

        def chunk(c):
            return pl.ds(pl.multiple_of(c * wide, wide), wide)

        def copies_in(c):
            return (
                pltpu.make_async_copy(cum_hbm.at[:, chunk(c)], cum_s.at[:, chunk(c)], cum_sem.at[c]),
                pltpu.make_async_copy(y_hbm.at[:, chunk(c)], y_s.at[:, chunk(c)], y_sem.at[c]),
                pltpu.make_async_copy(gate_hbm.at[:, chunk(c)], gate_s.at[:, chunk(c)], gate_sem.at[c]),
            )

        def copy_out(c):
            return pltpu.make_async_copy(out_s.at[:, chunk(c)], out_hbm.at[:, chunk(c)], out_sem.at[c])

        copy_a = pltpu.make_async_copy(a_hbm, a_ref, a_sem.at[0])
        copy_a.start()
        for c in range(min(AHEAD, chunks)):
            for copy in copies_in(c):
                copy.start()
        c_s[...] = spread_c(bc_ref[:, states:], states, False)
        copy_a.wait()

        def strip(j, _):
            lanes = at(j)
            strips = [
                h_ref[j * per_block + p, s * states : (s + 1) * states, :].astype(F32)
                for p in range(per_block)
                for s in range(share.strips)
            ]
            h_in = jnp.concatenate(strips, axis=1)
            rates = a_ref[:, lanes] * (-LOG2E)
            a_n = [jnp.broadcast_to(rates[n : n + 1], (GROUP, block)).astype(BF16) for n in range(states)]
            h_n = [jnp.broadcast_to(h_in[n : n + 1], (GROUP, block)).astype(BF16) for n in range(states)]
            for g in range(rows // GROUP):
                tokens = slice(g * GROUP, (g + 1) * GROUP)
                cum = cum_s[tokens, lanes]
                parts = [jnp.exp2(cum * a_n[n]) * h_n[n] for n in range(states)]
                fixed = jnp.dot(c_s[tokens, :], jnp.concatenate(parts, axis=0), preferred_element_type=F32)
                gate = gate_s[tokens, lanes].astype(F32)
                out_s[tokens, lanes] = ((y_s[tokens, lanes] + fixed) * silu(gate)).astype(BF16)
            return 0

        def run_chunk(c, _):
            for copy in copies_in(c):
                copy.wait()

            @pl.when(c + AHEAD < chunks)
            def _():
                for copy in copies_in(c + AHEAD):
                    copy.start()

            lax.fori_loop(c * ratio, (c + 1) * ratio, strip, 0)
            copy_out(c).start()
            return 0

        lax.fori_loop(0, chunks, run_chunk, 0)
        for c in range(chunks):
            copy_out(c).wait()

    whole = pl.BlockSpec(memory_space=pltpu.VMEM)
    held = pl.BlockSpec(memory_space=pltpu.HBM)
    return pl.pallas_call(
        body,
        in_specs=[held, whole, held, held, whole, held],
        out_specs=held,
        out_shape=jax.ShapeDtypeStruct((rows, width), BF16),
        scratch_shapes=[
            pltpu.VMEM((rows, width), BF16),
            pltpu.VMEM((rows, width), F32),
            pltpu.VMEM((rows, width), BF16),
            pltpu.VMEM((rows, width), BF16),
            pltpu.VMEM((states, width), F32),
            pltpu.VMEM((rows, GROUP * states), BF16),
        ]
        + [pltpu.SemaphoreType.DMA((chunks,))] * 4
        + [pltpu.SemaphoreType.DMA((1,))],
        compiler_params=pltpu.CompilerParams(vmem_limit_bytes=VMEM_BYTES),
        name="final",
    )(cum, h_in, y, gate, bc, decay)


def local(x_in, gate_in, conv_weight, conv_bias, x_proj, dt_proj, dt_bias, decay_rates, skip_gain):
    rows, width = x_in.shape
    taps = conv_weight.shape[0]
    states = decay_rates.shape[0]
    parts = lax.axis_size(AXES)
    share = Share(width, parts, states)
    prior = lax.ppermute(x_in[rows - (taps - 1) :], AXES, [(p, p + 1) for p in range(parts - 1)])
    mine = lax.axis_index(AXES).astype(jnp.int32)
    y, cum, message, bc = front(
        x_in, prior, conv_weight, conv_bias[None], x_proj.T, dt_proj, dt_bias[None], decay_rates, skip_gain[None], share
    )
    got = lax.all_to_all(message, AXES, 0, 0, tiled=True)
    incoming = combine(got, decay_rates, mine, share)
    h_in = lax.all_to_all(incoming, AXES, 0, 0, tiled=True)
    return final(cum, h_in, y, gate_in, bc, decay_rates, share)


def solution(mesh):
    split = P(AXES, None)
    return jax.shard_map(
        local,
        mesh=mesh,
        in_specs=(split, split, P(), P(), P(), P(), P(), P(), P()),
        out_specs=split,
        check_vma=False,
    )
```
